32 devices in a mesh: dom: 8 (over z, y), rhs: 4 (over x, core).
Axes of the slice: x: 2, y: 2, z: 4, core: 2. Of those that a mesh axis runs over, the one named last changes fastest.
Arguments:
- tile_values: float32 [2048, 128, 128], P(('dom', 'rhs')), may hold values from -1 to 3, as said below
- tile_rows: int32 [2048], P(('dom', 'rhs')), may hold values from -1 to 31, as said below
- tile_cols: int32 [2048], P(('dom', 'rhs')), may hold values from 0 to 39, as said below
- send_lists: int32 [8, 2, 4], P('dom'), may hold values from 0 to 31, as said below
- replace_flags: int32 [4], replicated, may hold values from 0 to 1, as said below
- right_side: float32 [4, 256, 128], P(None, ('dom', 'rhs')), may hold values from -25 to 25
- start_iterate: float32 [4, 256, 128], P(None, ('dom', 'rhs')), may hold values from -25 to 25
- start_residual: float32 [4, 256, 128], P(None, ('dom', 'rhs')), may hold values from -25 to 25
- start_direction: float32 [4, 256, 128], P(None, ('dom', 'rhs')), may hold values from -25 to 25
Outputs:
- new_iterate: float32 [4, 256, 128], P(None, ('dom', 'rhs'))
- new_residual: float32 [4, 256, 128], P(None, ('dom', 'rhs'))
- new_direction: float32 [4, 256, 128], P(None, ('dom', 'rhs'))
The draws below stay inside these ranges and needn't reach their ends.
Inputs may be any that keep to these rules, and one draw needn't show every extreme that they name: `tile_values`: the matrix assembled from all used tile slots is symmetric positive definite. `tile_rows`: -1 marks an empty slot; a used slot of the device with indices (d, r) names a block row from r * 8 to (r + 1) * 8 - 1 of partition d. `tile_cols`: 0 in empty slots. `send_lists`: the 8 entries of one partition are distinct. `replace_flags`: at least one load case is flagged and at least one is not.
All inputs are finite; a program needn't handle non-finite values.
Results may differ from the reference program's by a relative error of at most 0.0003.
Values sent between devices are 32-bit elements; how exact they have to be, the bound alone decides.
A program may use at most 64 MiB of HBM per device.

```python
import jax
import jax.numpy as jnp
import numpy as np
from jax import lax

TB = 128
NC = 4
SSTEP = 3
MATCH = 6
BP_DEV = 8
GH = 4
TCAP = 64
PARTS_SIZE = 8
SPLIT = 4
BP = 32
NB = 256
TILES = 2048


COUPLING = 0.25


def hadamard_table(order_size):
    indices = np.arange(order_size)
    crossed = indices[:, None] & indices[None, :]
    parity = np.zeros((order_size, order_size), np.int64)
    for bit_index in range(max(order_size.bit_length(), 1)):
        parity = parity ^ crossed >> bit_index & 1
    return (1 - 2 * parity).astype(np.float32)


def signed_basis(sub_key):
    key_perm, key_sign = jax.random.split(sub_key)
    hadamard = jnp.asarray(hadamard_table(TB)) / jnp.sqrt(jnp.float32(TB))
    permuted = hadamard[jax.random.permutation(key_perm, TB)]
    sign_flips = jax.random.randint(key_sign, (TB,), 0, 2).astype(jnp.float32) * 2.0 - 1.0
    return permuted * sign_flips[:, None]


def layout(key):
    base_key = jax.random.fold_in(key, 4242)
    key_active, key_force, key_heavy, key_sends, key_match = jax.random.split(base_key, 5)
    active = jax.random.randint(key_active, (PARTS_SIZE,), 0, MATCH + 1)
    forced = jax.random.randint(key_force, (), 0, PARTS_SIZE)
    active = active.at[forced].set(MATCH)
    heavy_device = jax.random.randint(key_heavy, (PARTS_SIZE,), 0, SPLIT)
    heavy_device = heavy_device.at[forced].set(SPLIT - 1)
    heavy_device = heavy_device.at[(forced + 1) % PARTS_SIZE].set(0)
    shuffled = jax.vmap(lambda part_key: jax.random.permutation(part_key, BP_DEV))(jax.random.split(key_sends, PARTS_SIZE))
    send_lists = (heavy_device[:, None] * BP_DEV + shuffled[:, :2 * GH]).reshape(PARTS_SIZE, 2, GH).astype(jnp.int32)
    match_keys = jax.random.split(key_match, PARTS_SIZE * MATCH)
    pairing = jax.vmap(lambda part_key: jax.random.permutation(part_key, BP))(match_keys).reshape(PARTS_SIZE, MATCH, BP)
    return (active, heavy_device, send_lists, pairing)


def slot_tables(key):
    active, heavy_device, send_lists, pairing = layout(key)
    part_ids = jnp.arange(PARTS_SIZE)[:, None, None]
    device_ids = jnp.arange(SPLIT)[None, :, None]
    slot_ids = jnp.arange(TCAP)[None, None, :]
    inverse = jnp.argsort(pairing, axis=-1)
    slot_local = slot_ids % BP_DEV
    own_row = device_ids * BP_DEV + slot_local
    match_index = jnp.clip(slot_ids // BP_DEV - 1, 0, MATCH - 1)
    position = inverse[part_ids, match_index, own_row]
    partner = pairing[part_ids, match_index, jnp.bitwise_xor(position, 1)]
    ghost_base = BP_DEV * (1 + MATCH)
    ghost_slot = jnp.clip(slot_ids - ghost_base, 0, 2 * GH - 1)
    ghost_side = ghost_slot // GH
    ghost_index = ghost_slot % GH
    ghost_row = send_lists[part_ids, ghost_side, ghost_index]
    is_diag = slot_ids < BP_DEV
    is_match = (slot_ids >= BP_DEV) & (slot_ids < ghost_base)
    is_ghost = slot_ids >= ghost_base
    match_live = is_match & (match_index < active[part_ids])
    has_side = jnp.where(ghost_side == 0, part_ids > 0, part_ids < PARTS_SIZE - 1)
    ghost_live = is_ghost & (device_ids == heavy_device[part_ids]) & has_side
    row_table = jnp.where(is_diag | match_live, own_row, jnp.where(ghost_live, ghost_row, -1))
    col_table = jnp.where(is_diag, own_row, jnp.where(match_live, partner, jnp.where(ghost_live, BP + ghost_slot, 0)))
    slot_kind = jnp.where(is_diag, 0, jnp.where(is_match, 1, 2))
    pair_id = jnp.where(is_match, (part_ids * MATCH + match_index) * BP + position // 2, (part_ids + ghost_side) * GH + ghost_index)
    pair_id = jnp.where(is_diag, part_ids * BP + own_row, pair_id)
    flipped = jnp.where(is_match, position % 2 == 1, ghost_side == 0)
    block_ids = jnp.arange(BP)
    part_line = jnp.arange(PARTS_SIZE)
    left_hits = jnp.sum(send_lists[:, 0, :, None] == block_ids, axis=1) * (part_line > 0)[:, None]
    right_hits = jnp.sum(send_lists[:, 1, :, None] == block_ids, axis=1) * (part_line < PARTS_SIZE - 1)[:, None]
    incidence = active[:, None] + left_hits + right_hits
    shape_all = (PARTS_SIZE, SPLIT, TCAP)
    return (jnp.broadcast_to(row_table, shape_all).astype(jnp.int32), jnp.broadcast_to(col_table, shape_all).astype(jnp.int32), jnp.broadcast_to(slot_kind, shape_all).astype(jnp.int32), jnp.broadcast_to(pair_id, shape_all).astype(jnp.int32), jnp.broadcast_to(flipped, shape_all), incidence)


def draw_tile_values(key, part):
    row_table, col_table, slot_kind, pair_id, flipped, incidence = slot_tables(key)
    value_key = jax.random.fold_in(key, 777)

    def one_slot(kind_value, id_value, flip_value, incidence_value):
        sub_key = jax.random.fold_in(jax.random.fold_in(value_key, kind_value), id_value)
        key_left, key_right, key_gain, key_extra = jax.random.split(sub_key, 4)
        left_basis = signed_basis(key_left)
        right_basis = jnp.where(kind_value == 0, left_basis, signed_basis(key_right))
        gain_values = jax.random.uniform(key_gain, (TB,), jnp.float32)
        gain_values = jnp.where(kind_value == 0, 2.0 * gain_values - 1.0, 0.3 + 0.7 * gain_values)
        tile_value = COUPLING * jnp.dot(left_basis * gain_values[None, :], right_basis.T, precision=lax.Precision.HIGHEST)
        tile_value = jnp.where(flip_value, tile_value.T, tile_value)
        extra_diag = jnp.exp(jax.random.uniform(key_extra, (TB,), jnp.float32, jnp.log(0.05), jnp.log(0.5)))
        diagonal = COUPLING * (incidence_value + 1.0) + extra_diag
        return tile_value + jnp.where(kind_value == 0, 1.0, 0.0) * jnp.diag(diagonal)

    def one_part(packed):
        part_kind, part_id, part_flip, part_rows, part_incidence = packed
        slot_incidence = part_incidence[jnp.clip(part_rows, 0, BP - 1)].astype(jnp.float32)
        return jax.vmap(one_slot)(part_kind, part_id, part_flip, slot_incidence)
    tile_stack = lax.map(one_part, (slot_kind.reshape(PARTS_SIZE, SPLIT * TCAP), pair_id.reshape(PARTS_SIZE, SPLIT * TCAP), flipped.reshape(PARTS_SIZE, SPLIT * TCAP), row_table.reshape(PARTS_SIZE, SPLIT * TCAP), incidence))
    return tile_stack.reshape(TILES, TB, TB)


def draw_tile_rows(key, part):
    return slot_tables(key)[0].reshape(TILES)


def draw_tile_cols(key, part):
    return slot_tables(key)[1].reshape(TILES)


def draw_send_lists(key, part):
    return layout(key)[2]


def draw_replace_flags(key, part):
    flag_key = jax.random.fold_in(key, 31)
    key_perm, key_count = jax.random.split(flag_key)
    ranking = jax.random.permutation(key_perm, NC)
    flagged_count = jax.random.randint(key_count, (), 1, NC)
    return (ranking < flagged_count).astype(jnp.int32)


def vector_draw(key, salt):
    sub_key = jax.random.fold_in(key, salt)
    key_noise, key_scale = jax.random.split(sub_key, 2)
    part_ramp = 1.0 + 2.0 * jnp.arange(PARTS_SIZE, dtype=jnp.float32) / max(PARTS_SIZE - 1, 1)
    block_ramp = jnp.repeat(part_ramp, BP)
    row_scale = jnp.exp(jax.random.uniform(key_scale, (NC, NB, 1), jnp.float32, jnp.log(0.4), jnp.log(1.2)))
    row_scale = row_scale * block_ramp[None, :, None]
    noise_part = jax.random.normal(key_noise, (NC, NB, TB), jnp.float32)
    return row_scale * noise_part


def draw_right_side(key, part):
    return vector_draw(key, 11)


def draw_start_iterate(key, part):
    return vector_draw(key, 12)


def draw_start_residual(key, part):
    return vector_draw(key, 13)


def draw_start_direction(key, part):
    return vector_draw(key, 14)


def setup_inputs(seed: int = 0) -> dict:
    key_list = jax.random.split(jax.random.key(seed), 10)
    tile_values = draw_tile_values(jax.random.fold_in(key_list[9], 71), 0)
    tile_rows = draw_tile_rows(jax.random.fold_in(key_list[9], 71), 0)
    tile_cols = draw_tile_cols(jax.random.fold_in(key_list[9], 71), 0)
    send_lists = draw_send_lists(jax.random.fold_in(key_list[9], 71), 0)
    replace_flags = draw_replace_flags(jax.random.fold_in(key_list[9], 71), 0)
    right_side = draw_right_side(jax.random.fold_in(key_list[9], 71), 0)
    start_iterate = draw_start_iterate(jax.random.fold_in(key_list[9], 71), 0)
    start_residual = draw_start_residual(jax.random.fold_in(key_list[9], 71), 0)
    start_direction = draw_start_direction(jax.random.fold_in(key_list[9], 71), 0)
    return dict(tile_values=tile_values, tile_rows=tile_rows, tile_cols=tile_cols, send_lists=send_lists, replace_flags=replace_flags, right_side=right_side, start_iterate=start_iterate, start_residual=start_residual, start_direction=start_direction)


highest = lax.Precision.HIGHEST


def shift_table(basis_steps):
    basis_width = 2 * basis_steps + 1
    shift_matrix = np.zeros((basis_width, basis_width), np.float32)
    for position in range(basis_steps):
        shift_matrix[position + 1, position] = 1.0
    for position in range(basis_steps - 1):
        shift_matrix[basis_steps + 2 + position, basis_steps + 1 + position] = 1.0
    return shift_matrix


def coefficients(gram_matrix, basis_steps):
    shift_matrix = jnp.asarray(shift_table(basis_steps))
    case_count = gram_matrix.shape[0]
    basis_width = gram_matrix.shape[1]
    eye_matrix = jnp.eye(basis_width, dtype=jnp.float32)
    direction = jnp.broadcast_to(eye_matrix[0], (case_count, basis_width))
    residual = jnp.broadcast_to(eye_matrix[basis_steps + 1], (case_count, basis_width))
    iterate = jnp.zeros((case_count, basis_width), jnp.float32)

    def quadratic(first_vec, second_vec):
        return jnp.einsum('ci,cij,cj->c', first_vec, gram_matrix, second_vec, precision=highest)

    res_norm = quadratic(residual, residual)
    for inner_step in range(basis_steps):
        mapped = jnp.einsum('ij,cj->ci', shift_matrix, direction, precision=highest)
        step_size = res_norm / quadratic(direction, mapped)
        iterate = iterate + step_size[:, None] * direction
        residual = residual - step_size[:, None] * mapped
        next_norm = quadratic(residual, residual)
        direction = residual + (next_norm / res_norm)[:, None] * direction
        res_norm = next_norm
    return iterate, residual, direction


def combine(basis_stack, weights):
    return jnp.einsum('icbt,ci->cbt', basis_stack, weights, precision=highest)


def spread_ghosts(blocks, send_lists):
    flat_sends = send_lists.reshape(PARTS_SIZE, 2 * GH)
    picked = jax.vmap(lambda part_blocks, part_sends: jnp.take(part_blocks, part_sends, axis=2),
                      in_axes=(2, 0), out_axes=2)(blocks, flat_sends)
    to_left = picked[:, :, :, :GH]
    to_right = picked[:, :, :, GH:]
    zero_part = jnp.zeros_like(to_left[:, :, :1])
    from_left = jnp.concatenate([zero_part, to_right[:, :, :-1]], axis=2)
    from_right = jnp.concatenate([to_left[:, :, 1:], zero_part], axis=2)
    return jnp.concatenate([blocks, from_left, from_right], axis=3)


def apply_matrix(vectors, tile_values, tile_rows, tile_cols, send_lists):
    stack_count = vectors.shape[0]
    blocks = vectors.reshape(stack_count, NC, PARTS_SIZE, BP, TB)
    extended = spread_ghosts(blocks, send_lists)
    part_tiles = tile_values.reshape(PARTS_SIZE, SPLIT * TCAP, TB, TB)
    part_rows = tile_rows.reshape(PARTS_SIZE, SPLIT * TCAP)
    part_cols = tile_cols.reshape(PARTS_SIZE, SPLIT * TCAP)

    def one_part(packed):
        ext_part, tile_part, row_part, col_part = packed
        picked = jnp.take(ext_part, col_part, axis=2)
        product = jnp.einsum('tij,kctj->kcti', tile_part, picked, precision=highest)
        wanted = lax.iota(jnp.int32, BP)
        onehot = (row_part[:, None] == wanted[None, :]).astype(jnp.float32)
        return jnp.einsum('tb,kcti->kcbi', onehot, product, precision=highest)

    result = lax.map(one_part, (jnp.moveaxis(extended, 2, 0), part_tiles, part_rows, part_cols))
    return jnp.moveaxis(result, 0, 2).reshape(stack_count, NC, NB, TB)


def basis_from(apply_operator, direction, residual):
    direction_powers = [direction]
    residual_powers = [residual]
    for power_step in range(SSTEP):
        members = [direction_powers[-1]]
        if power_step < SSTEP - 1:
            members.append(residual_powers[-1])
        mapped = apply_operator(jnp.stack(members))
        direction_powers.append(mapped[0])
        if power_step < SSTEP - 1:
            residual_powers.append(mapped[1])
    return jnp.stack(direction_powers + residual_powers)


def reference(tile_values, tile_rows, tile_cols, send_lists, replace_flags, right_side, start_iterate, start_residual, start_direction):
    def apply_operator(vectors):
        return apply_matrix(vectors, tile_values, tile_rows, tile_cols, send_lists)

    basis_stack = basis_from(apply_operator, start_direction, start_residual)
    gram_matrix = jnp.einsum('icbt,jcbt->cij', basis_stack, basis_stack, precision=highest)
    iterate_coef, residual_coef, direction_coef = coefficients(gram_matrix, SSTEP)
    new_iterate = start_iterate + combine(basis_stack, iterate_coef)
    recursive = combine(basis_stack, residual_coef)
    new_direction = combine(basis_stack, direction_coef)
    replaced = right_side - apply_operator(new_iterate[None])[0]
    new_residual = jnp.where(replace_flags[:, None, None] > 0, replaced, recursive)
    return new_iterate, new_residual, new_direction
```

```python
import functools

import jax
import jax.numpy as jnp
from jax import lax
from jax.experimental import pallas as pl
from jax.experimental.pallas import tpu as pltpu
from jax.sharding import PartitionSpec as P

SSTEP = 3
WIDTH = 2 * SSTEP + 1
P0, R0, X0, P1, R1, P2 = range(6)
SENT = 6
MESH = pl.DeviceIdType.MESH
UNROLL = 4
PAIRS = [(i, j) for i in range(WIDTH) for j in range(i, WIDTH)]
PAIR_LANE = {pair: lane for lane, pair in enumerate(PAIRS)}


def shifted_of(vec):
    return {i + 1: v for i, v in vec.items() if i not in (SSTEP, WIDTH - 1)}


def axpy(base, scale, other, sign):
    out = dict(base)
    for i, v in other.items():
        term = scale * v
        if i in out:
            out[i] = out[i] + term if sign > 0 else out[i] - term
        else:
            out[i] = term if sign > 0 else -term
    return out


def coefficients(gram):
    def quadratic(first, second):
        total = None
        for i, a in first.items():
            inner = None
            for j, b in second.items():
                term = gram[(min(i, j), max(i, j))] * b
                inner = term if inner is None else inner + term
            inner = inner * a
            total = inner if total is None else total + inner
        return total

    one = jnp.ones_like(gram[(0, 0)])
    direction = {0: one}
    residual = {SSTEP + 1: one}
    iterate = {}
    norm = quadratic(residual, residual)
    for _ in range(SSTEP):
        mapped = shifted_of(direction)
        step = norm / quadratic(direction, mapped)
        iterate = axpy(iterate, step, direction, 1)
        residual = axpy(residual, step, mapped, -1)
        next_norm = quadratic(residual, residual)
        direction = axpy(residual, next_norm / norm, direction, 1)
        norm = next_norm
    return iterate, residual, direction


def kernel(
    parts,
    split,
    rows_s,
    cols_s,
    sends_s,
    flags_s,
    tiles_h,
    right_h,
    iterate_h,
    residual_h,
    direction_h,
    iterate_o,
    residual_o,
    direction_o,
    *scratch,
):
    scratch = list(scratch)
    take = lambda n: [scratch.pop(0) for _ in range(n)]
    ext = take(SENT)
    own = take(SENT + 3)
    ghost_send = take(SENT)
    ghost_recv = take(SENT)
    tiles, weights, vec_in, gram_r, gram_d = take(5)
    tile_sem, vec_sem, peer_send, peer_recv, side_send, side_recv = take(6)
    gr_send, gr_recv, gd_send, gd_recv = take(4)

    d, r = lax.axis_index("dom"), lax.axis_index("rhs")
    cases, own_rows, tb = own[0].shape[1], own[0].shape[0], own[0].shape[2]
    gh = ghost_send[0].shape[1]
    tile_count = tiles.shape[0]
    chunks = tile_sem.shape[0]
    per_chunk = tile_count // chunks
    base = r * own_rows
    has_left, has_right = d > 0, d < parts - 1

    vec_copies = []
    for i, ref in enumerate((direction_h, residual_h, iterate_h, right_h)):
        copy = pltpu.make_async_copy(ref, vec_in.at[i], vec_sem.at[i])
        copy.start()
        vec_copies.append(copy)
    tile_copies = []
    for i in range(chunks):
        part = pl.ds(i * per_chunk, per_chunk)
        copy = pltpu.make_async_copy(tiles_h.at[part], tiles.at[part], tile_sem.at[i])
        copy.start()
        tile_copies.append(copy)

    barrier = pltpu.get_barrier_semaphore()

    def greet(dd, rr):
        pl.semaphore_signal(barrier, inc=1, device_id=(dd, rr), device_id_type=MESH)

    for o in range(1, split):
        greet(d, lax.rem(r + o, split))

    @pl.when(has_left)
    def _():
        for o in range(1, split):
            greet(d - 1, lax.rem(r + o, split))

    @pl.when(has_right)
    def _():
        for o in range(1, split):
            greet(d + 1, lax.rem(r + o, split))

    @pl.loop(1, parts)
    def _(o):
        greet(lax.rem(d + o, parts), r)

    sides = has_left.astype(jnp.int32) + has_right.astype(jnp.int32)

    def peer_copy(v, o):
        return pltpu.make_async_remote_copy(
            src_ref=own[v],
            dst_ref=ext[v].at[pl.ds(base, own_rows)],
            send_sem=peer_send.at[v, o - 1],
            recv_sem=peer_recv.at[v, o - 1],
            device_id=(d, lax.rem(r + o, split)),
            device_id_type=MESH,
        )

    def side_copy(v, side, o):
        return pltpu.make_async_remote_copy(
            src_ref=ghost_send[v].at[side],
            dst_ref=ghost_recv[v].at[1 - side, o],
            send_sem=side_send.at[v, side, o],
            recv_sem=side_recv.at[v, 1 - side, o],
            device_id=(d - 1 if side == 0 else d + 1, lax.rem(r + o, split)),
            device_id_type=MESH,
        )

    def stage(v, values):
        for b in range(own_rows):
            own[v][b] = values[b]
            ext[v][base + b] = values[b]
        for side in range(2):
            for k in range(gh):
                local = sends_s[0, side, k] - base
                value = own[v][jnp.clip(local, 0, own_rows - 1)]
                where = jnp.full((cases, tb), local, jnp.int32)
                ghost_send[v][side, k] = jnp.where(
                    (where >= 0) & (where < own_rows), value, 0.0
                )

    def send(v):
        @pl.when(has_left)
        def _():
            for o in range(split):
                side_copy(v, 0, o).start()

        @pl.when(has_right)
        def _():
            for o in range(split):
                side_copy(v, 1, o).start()

        for o in range(1, split):
            peer_copy(v, o).start()

    def receive(v):
        for o in range(1, split):
            peer_copy(v, o).wait_recv()
        for side, present in ((0, has_left), (1, has_right)):
            first = split * own_rows + side * gh

            @pl.when(present)
            def _():
                for o in range(split):
                    side_copy(v, 1 - side, o).wait_recv()
                for k in range(gh):
                    total = ghost_recv[v][side, 0, k]
                    for o in range(1, split):
                        total = total + ghost_recv[v][side, o, k]
                    ext[v][first + k] = total

            @pl.when(jnp.logical_not(present))
            def _():
                for k in range(gh):
                    ext[v][first + k] = jnp.zeros((cases, tb), jnp.float32)

    def sent(v):
        for o in range(1, split):
            peer_copy(v, o).wait_send()
        for side, present in ((0, has_left), (1, has_right)):

            @pl.when(present)
            def _():
                for o in range(split):
                    side_copy(v, side, o).wait_send()

    def input_blocks(i):
        return [vec_in[i, :, b, :] for b in range(own_rows)]

    low = lax.broadcasted_iota(jnp.int32, (2 * cases, tb), 0) < cases

    def apply_to(v):
        def step(i, acc):
            acc = list(acc)
            for u in range(UNROLL):
                q = i * UNROLL + u
                pair = jnp.concatenate(
                    [ext[v][cols_s[2 * q]], ext[v][cols_s[2 * q + 1]]], axis=0
                )
                high = pair.astype(jnp.bfloat16).astype(jnp.float32)
                lhs = jnp.concatenate([high, pair - high], axis=0).astype(jnp.bfloat16)
                lhs = jnp.concatenate([lhs, lhs], axis=1)
                out = jnp.dot(lhs, weights[q], preferred_element_type=jnp.float32)
                out = out[: 2 * cases] + out[2 * cases :]
                out = jnp.where(low, out[:, :tb], out[:, tb:])
                row = jnp.where(low, rows_s[2 * q], rows_s[2 * q + 1]) - base
                acc = [a + jnp.where(row == b, out, 0.0) for b, a in enumerate(acc)]
            return tuple(acc)

        zero = jnp.zeros((2 * cases, tb), jnp.float32)
        acc = lax.fori_loop(0, tile_count // 2 // UNROLL, step, (zero,) * own_rows)
        return [a[:cases] + a[cases:] for a in acc]

    for v in range(3):
        vec_copies[v].wait()
        stage(v, input_blocks(v))
    pl.semaphore_wait(barrier, split - 1 + parts - 1 + (split - 1) * sides)
    for v in range(3):
        send(v)

    for i in range(chunks):
        tile_copies[i].wait()

        @pl.loop(i * per_chunk // 2, (i + 1) * per_chunk // 2)
        def _(q):
            for h in range(2):
                flipped = tiles[2 * q + h].T
                high = flipped.astype(jnp.bfloat16)
                weights[q, :tb, h * tb : (h + 1) * tb] = high
                weights[q, tb:, h * tb : (h + 1) * tb] = (
                    flipped - high.astype(jnp.float32)
                ).astype(jnp.bfloat16)

    lanes = lax.broadcasted_iota(jnp.int32, (cases, tb), 1)
    basis = [own[P0], own[P1], own[P2], own[SENT], own[R0], own[R1], own[SENT + 1]]
    image = own[SENT + 2]

    def gram_of(payload, pairs):
        for i, j in pairs:
            total = basis[i][0] * basis[j][0]
            for b in range(1, own_rows):
                total = total + basis[i][b] * basis[j][b]
            total = jnp.sum(total, axis=1, keepdims=True)
            payload = payload + jnp.where(lanes == PAIR_LANE[(i, j)], total, 0.0)
        return payload

    def pairs_new(known, new):
        have = set(known) | set(new)
        return [p for p in PAIRS if set(p) <= have and set(p) & set(new)]

    receive(P0)
    stage(P1, apply_to(P0))
    send(P1)
    receive(R0)
    stage(R1, apply_to(R0))
    send(R1)
    receive(X0)
    for b, value in enumerate(apply_to(X0)):
        image[b] = value
    payload = jnp.zeros((cases, tb), jnp.float32)
    payload = gram_of(payload, pairs_new([], [0, 1, 4, 5]))
    receive(P1)
    stage(P2, apply_to(P1))
    send(P2)
    receive(R1)
    for b, value in enumerate(apply_to(R1)):
        own[SENT + 1][b] = value
    payload = gram_of(payload, pairs_new([0, 1, 4, 5], [2, 6]))
    receive(P2)
    for b, value in enumerate(apply_to(P2)):
        own[SENT][b] = value
    payload = gram_of(payload, pairs_new([0, 1, 2, 4, 5, 6], [3]))

    gram_r[r] = payload

    def gram_r_copy(o):
        return pltpu.make_async_remote_copy(
            src_ref=gram_r.at[r],
            dst_ref=gram_r.at[r],
            send_sem=gr_send.at[o - 1],
            recv_sem=gr_recv.at[o - 1],
            device_id=(d, lax.rem(r + o, split)),
            device_id_type=MESH,
        )

    for o in range(1, split):
        gram_r_copy(o).start()
    for o in range(1, split):
        gram_r_copy(o).wait()
    gram_d[d] = jnp.sum(gram_r[...], axis=0)

    def gram_d_copy(o):
        return pltpu.make_async_remote_copy(
            src_ref=gram_d.at[d],
            dst_ref=gram_d.at[d],
            send_sem=gd_send.at[o - 1],
            recv_sem=gd_recv.at[o - 1],
            device_id=(lax.rem(d + o, parts), r),
            device_id_type=MESH,
        )

    @pl.loop(1, parts)
    def _(o):
        gram_d_copy(o).start()

    for v in range(SENT):
        sent(v)
    vec_copies[3].wait()

    @pl.loop(1, parts)
    def _(o):
        gram_d_copy(o).wait()

    whole = jnp.sum(gram_d[...], axis=0)
    gram = {
        pair: jnp.broadcast_to(whole[:, lane : lane + 1], (cases, tb))
        for pair, lane in PAIR_LANE.items()
    }
    iterate_c, residual_c, direction_c = coefficients(gram)
    shifted_c = shifted_of(iterate_c)
    case_ids = lax.broadcasted_iota(jnp.int32, (cases, tb), 0)
    flags = jnp.zeros((cases, tb), jnp.int32)
    for c in range(cases):
        flags = jnp.where(case_ids == c, flags_s[c], flags)

    for b in range(own_rows):
        blocks = [ref[b] for ref in basis]

        def combine(weights_of):
            total = None
            for i, w in weights_of.items():
                total = blocks[i] * w if total is None else total + blocks[i] * w
            return total

        replaced = vec_in[3, :, b, :] - (image[b] + combine(shifted_c))
        iterate_o[:, b, :] = vec_in[2, :, b, :] + combine(iterate_c)
        residual_o[:, b, :] = jnp.where(flags > 0, replaced, combine(residual_c))
        direction_o[:, b, :] = combine(direction_c)


def body(parts, split, tiles, rows, cols, sends, flags, right, iterate, residual, direction):
    cases, own_rows, tb = residual.shape
    gh = sends.shape[2]
    count = tiles.shape[0]
    f32 = jnp.float32
    dma = pltpu.SemaphoreType.DMA
    smem = pl.BlockSpec(memory_space=pltpu.SMEM)
    hbm = pl.BlockSpec(memory_space=pl.ANY)
    vmem = pl.BlockSpec(memory_space=pltpu.VMEM)
    scratch = (
        [pltpu.VMEM((split * own_rows + 2 * gh, cases, tb), f32)] * SENT
        + [pltpu.VMEM((own_rows, cases, tb), f32)] * (SENT + 3)
        + [pltpu.VMEM((2, gh, cases, tb), f32)] * SENT
        + [pltpu.VMEM((2, split, gh, cases, tb), f32)] * SENT
        + [
            pltpu.VMEM((count, tb, tb), f32),
            pltpu.VMEM((count // 2, 2 * tb, 2 * tb), jnp.bfloat16),
            pltpu.VMEM((4, cases, own_rows, tb), f32),
            pltpu.VMEM((split, cases, tb), f32),
            pltpu.VMEM((parts, cases, tb), f32),
            dma((4,)),
            dma((4,)),
            dma((SENT, split - 1)),
            dma((SENT, split - 1)),
            dma((SENT, 2, split)),
            dma((SENT, 2, split)),
            dma((split - 1,)),
            dma((split - 1,)),
            dma((parts - 1,)),
            dma((parts - 1,)),
        ]
    )
    out = jax.ShapeDtypeStruct((cases, own_rows, tb), f32)
    return pl.pallas_call(
        functools.partial(kernel, parts, split),
        out_shape=(out, out, out),
        in_specs=[smem] * 4 + [hbm] * 5,
        out_specs=(vmem, vmem, vmem),
        scratch_shapes=scratch,
        compiler_params=pltpu.CompilerParams(
            collective_id=0, has_side_effects=True, vmem_limit_bytes=40 * 1024 * 1024
        ),
    )(rows, cols, sends, flags, tiles, right, iterate, residual, direction)


def solution(mesh):
    both = ("dom", "rhs")
    vec = P(None, both, None)
    placed = (P(both, None, None), P(both), P(both), P("dom", None, None), P(), vec, vec, vec, vec)
    return jax.shard_map(
        functools.partial(body, mesh.shape["dom"], mesh.shape["rhs"]),
        mesh=mesh,
        in_specs=placed,
        out_specs=(vec, vec, vec),
        check_vma=False,
    )
```

```python
import functools

import jax
import jax.numpy as jnp
from jax import lax
from jax.experimental import pallas as pl
from jax.experimental.pallas import tpu as pltpu
from jax.sharding import PartitionSpec as P

SSTEP = 3
WIDTH = 2 * SSTEP + 1
P0, R0, X0, P1, R1, P2 = range(6)
SENT = 6
MESH = pl.DeviceIdType.MESH
UNROLL = 16
PAIRS = [(i, j) for i in range(WIDTH) for j in range(i, WIDTH)]
PAIR_LANE = {pair: lane for lane, pair in enumerate(PAIRS)}


def shifted_of(vec):
    return {i + 1: v for i, v in vec.items() if i not in (SSTEP, WIDTH - 1)}


def axpy(base, scale, other, sign):
    out = dict(base)
    for i, v in other.items():
        term = scale * v
        if i in out:
            out[i] = out[i] + term if sign > 0 else out[i] - term
        else:
            out[i] = term if sign > 0 else -term
    return out


def coefficients(gram):
    def quadratic(first, second):
        total = None
        for i, a in first.items():
            inner = None
            for j, b in second.items():
                term = gram[(min(i, j), max(i, j))] * b
                inner = term if inner is None else inner + term
            inner = inner * a
            total = inner if total is None else total + inner
        return total

    one = jnp.ones_like(gram[(0, 0)])
    direction = {0: one}
    residual = {SSTEP + 1: one}
    iterate = {}
    norm = quadratic(residual, residual)
    for _ in range(SSTEP):
        mapped = shifted_of(direction)
        step = norm / quadratic(direction, mapped)
        iterate = axpy(iterate, step, direction, 1)
        residual = axpy(residual, step, mapped, -1)
        next_norm = quadratic(residual, residual)
        direction = axpy(residual, next_norm / norm, direction, 1)
        norm = next_norm
    return iterate, residual, direction


def kernel(
    parts,
    split,
    rows_s,
    cols_s,
    sends_s,
    tiles_h,
    iterate_h,
    residual_h,
    direction_h,
    out_ref,
    *scratch,
):
    scratch = list(scratch)
    take = lambda n: [scratch.pop(0) for _ in range(n)]
    ext = take(SENT)
    own = take(SENT + 3)
    ghost_send = take(SENT)
    ghost_recv = take(SENT)
    tiles, weights, vec_in, gram_r, gram_d = take(5)
    tile_sem, vec_sem, peer_send, peer_recv, side_send, side_recv = take(6)
    gr_send, gr_recv, gd_send, gd_recv = take(4)

    d, r = lax.axis_index("dom"), lax.axis_index("rhs")
    cases, own_rows, tb = own[0].shape[1], own[0].shape[0], own[0].shape[2]
    gh = ghost_send[0].shape[1]
    tile_count = tiles.shape[0]
    chunks = tile_sem.shape[0]
    per_chunk = tile_count // chunks
    base = r * own_rows
    has_left, has_right = d > 0, d < parts - 1

    vec_copies = []
    for i, ref in enumerate((direction_h, residual_h, iterate_h)):
        copy = pltpu.make_async_copy(ref, vec_in.at[i], vec_sem.at[i])
        copy.start()
        vec_copies.append(copy)
    tile_copies = []
    for i in range(chunks):
        part = pl.ds(i * per_chunk, per_chunk)
        copy = pltpu.make_async_copy(tiles_h.at[part], tiles.at[part], tile_sem.at[i])
        copy.start()
        tile_copies.append(copy)

    barrier = pltpu.get_barrier_semaphore()

    def greet(dd, rr):
        pl.semaphore_signal(barrier, inc=1, device_id=(dd, rr), device_id_type=MESH)

    for o in range(1, split):
        greet(d, lax.rem(r + o, split))

    @pl.when(has_left)
    def _():
        for o in range(1, split):
            greet(d - 1, lax.rem(r + o, split))

    @pl.when(has_right)
    def _():
        for o in range(1, split):
            greet(d + 1, lax.rem(r + o, split))

    @pl.loop(1, parts)
    def _(o):
        greet(lax.rem(d + o, parts), r)

    sides = has_left.astype(jnp.int32) + has_right.astype(jnp.int32)

    def peer_copy(v, o):
        return pltpu.make_async_remote_copy(
            src_ref=own[v],
            dst_ref=ext[v].at[pl.ds(base, own_rows)],
            send_sem=peer_send.at[v, o - 1],
            recv_sem=peer_recv.at[v, o - 1],
            device_id=(d, lax.rem(r + o, split)),
            device_id_type=MESH,
        )

    def side_copy(v, side, o):
        return pltpu.make_async_remote_copy(
            src_ref=ghost_send[v].at[side],
            dst_ref=ghost_recv[v].at[1 - side, o],
            send_sem=side_send.at[v, side, o],
            recv_sem=side_recv.at[v, 1 - side, o],
            device_id=(d - 1 if side == 0 else d + 1, lax.rem(r + o, split)),
            device_id_type=MESH,
        )

    def stage(v, values):
        for b in range(own_rows):
            own[v][b] = values[b]
            ext[v][base + b] = values[b]
        for side in range(2):
            for k in range(gh):
                local = sends_s[0, side, k] - base
                value = own[v][jnp.clip(local, 0, own_rows - 1)]
                where = jnp.full((cases, tb), local, jnp.int32)
                ghost_send[v][side, k] = jnp.where(
                    (where >= 0) & (where < own_rows), value, 0.0
                )

    def send(v):
        @pl.when(has_left)
        def _():
            for o in range(split):
                side_copy(v, 0, o).start()

        @pl.when(has_right)
        def _():
            for o in range(split):
                side_copy(v, 1, o).start()

        for o in range(1, split):
            peer_copy(v, o).start()

    def receive(v):
        for o in range(1, split):
            peer_copy(v, o).wait_recv()
        for side, present in ((0, has_left), (1, has_right)):
            first = split * own_rows + side * gh

            @pl.when(present)
            def _():
                for o in range(split):
                    side_copy(v, 1 - side, o).wait_recv()
                for k in range(gh):
                    total = ghost_recv[v][side, 0, k]
                    for o in range(1, split):
                        total = total + ghost_recv[v][side, o, k]
                    ext[v][first + k] = total

            @pl.when(jnp.logical_not(present))
            def _():
                for k in range(gh):
                    ext[v][first + k] = jnp.zeros((cases, tb), jnp.float32)

    def sent(v):
        for o in range(1, split):
            peer_copy(v, o).wait_send()
        for side, present in ((0, has_left), (1, has_right)):

            @pl.when(present)
            def _():
                for o in range(split):
                    side_copy(v, side, o).wait_send()

    def input_blocks(i):
        return [vec_in[i, :, b, :] for b in range(own_rows)]

    low = lax.broadcasted_iota(jnp.int32, (2 * cases, tb), 0) < cases

    def apply_to(v):
        def step(i, acc):
            acc = list(acc)
            for u in range(UNROLL):
                q = i * UNROLL + u
                pair = jnp.concatenate(
                    [ext[v][cols_s[2 * q]], ext[v][cols_s[2 * q + 1]]], axis=0
                )
                high = pair.astype(jnp.bfloat16).astype(jnp.float32)
                lhs = jnp.concatenate([high, pair - high], axis=0).astype(jnp.bfloat16)
                lhs = jnp.concatenate([lhs, lhs], axis=1)
                out = jnp.dot(lhs, weights[q], preferred_element_type=jnp.float32)
                out = out[: 2 * cases] + out[2 * cases :]
                out = jnp.where(low, out[:, :tb], out[:, tb:])
                row = jnp.where(low, rows_s[2 * q], rows_s[2 * q + 1]) - base
                acc = [a + jnp.where(row == b, out, 0.0) for b, a in enumerate(acc)]
            return tuple(acc)

        zero = jnp.zeros((2 * cases, tb), jnp.float32)
        acc = lax.fori_loop(0, tile_count // 2 // UNROLL, step, (zero,) * own_rows)
        return [a[:cases] + a[cases:] for a in acc]

    for v in range(3):
        vec_copies[v].wait()
        stage(v, input_blocks(v))
    pl.semaphore_wait(barrier, split - 1 + parts - 1 + (split - 1) * sides)
    for v in range(3):
        send(v)

    for i in range(chunks):
        tile_copies[i].wait()

        @pl.loop(i * per_chunk // 2, (i + 1) * per_chunk // 2)
        def _(q):
            for h in range(2):
                flipped = tiles[2 * q + h].T
                high = flipped.astype(jnp.bfloat16)
                weights[q, :tb, h * tb : (h + 1) * tb] = high
                weights[q, tb:, h * tb : (h + 1) * tb] = (
                    flipped - high.astype(jnp.float32)
                ).astype(jnp.bfloat16)

    lanes = lax.broadcasted_iota(jnp.int32, (cases, tb), 1)
    basis = [own[P0], own[P1], own[P2], own[SENT], own[R0], own[R1], own[SENT + 1]]
    image = own[SENT + 2]

    def gram_of(payload, pairs):
        for i, j in pairs:
            total = basis[i][0] * basis[j][0]
            for b in range(1, own_rows):
                total = total + basis[i][b] * basis[j][b]
            total = jnp.sum(total, axis=1, keepdims=True)
            payload = payload + jnp.where(lanes == PAIR_LANE[(i, j)], total, 0.0)
        return payload

    def pairs_new(known, new):
        have = set(known) | set(new)
        return [p for p in PAIRS if set(p) <= have and set(p) & set(new)]

    receive(P0)
    stage(P1, apply_to(P0))
    send(P1)
    receive(R0)
    stage(R1, apply_to(R0))
    send(R1)
    receive(X0)
    for b, value in enumerate(apply_to(X0)):
        image[b] = value
    payload = jnp.zeros((cases, tb), jnp.float32)
    payload = gram_of(payload, pairs_new([], [0, 1, 4, 5]))
    receive(P1)
    stage(P2, apply_to(P1))
    send(P2)
    receive(R1)
    for b, value in enumerate(apply_to(R1)):
        own[SENT + 1][b] = value
    payload = gram_of(payload, pairs_new([0, 1, 4, 5], [2, 6]))
    receive(P2)
    for b, value in enumerate(apply_to(P2)):
        own[SENT][b] = value
    payload = gram_of(payload, pairs_new([0, 1, 2, 4, 5, 6], [3]))

    gram_r[r] = payload

    def gram_r_copy(o):
        return pltpu.make_async_remote_copy(
            src_ref=gram_r.at[r],
            dst_ref=gram_r.at[r],
            send_sem=gr_send.at[o - 1],
            recv_sem=gr_recv.at[o - 1],
            device_id=(d, lax.rem(r + o, split)),
            device_id_type=MESH,
        )

    for o in range(1, split):
        gram_r_copy(o).start()
    for o in range(1, split):
        gram_r_copy(o).wait()
    gram_d[d] = jnp.sum(gram_r[...], axis=0)

    def gram_d_copy(o):
        return pltpu.make_async_remote_copy(
            src_ref=gram_d.at[d],
            dst_ref=gram_d.at[d],
            send_sem=gd_send.at[o - 1],
            recv_sem=gd_recv.at[o - 1],
            device_id=(lax.rem(d + o, parts), r),
            device_id_type=MESH,
        )

    @pl.loop(1, parts)
    def _(o):
        gram_d_copy(o).start()

    for v in range(SENT):
        sent(v)

    @pl.loop(1, parts)
    def _(o):
        gram_d_copy(o).wait()

    whole = jnp.sum(gram_d[...], axis=0)
    gram = {
        pair: jnp.broadcast_to(whole[:, lane : lane + 1], (cases, tb))
        for pair, lane in PAIR_LANE.items()
    }
    iterate_c, residual_c, direction_c = coefficients(gram)
    shifted_c = shifted_of(iterate_c)
    for b in range(own_rows):
        blocks = [ref[b] for ref in basis]

        def combine(weights_of):
            total = None
            for i, w in weights_of.items():
                total = blocks[i] * w if total is None else total + blocks[i] * w
            return total

        out_ref[0, :, b, :] = combine(iterate_c)
        out_ref[1, :, b, :] = image[b] + combine(shifted_c)
        out_ref[2, :, b, :] = combine(residual_c)
        out_ref[3, :, b, :] = combine(direction_c)


def body(parts, split, tiles, rows, cols, sends, flags, right, iterate, residual, direction):
    cases, own_rows, tb = residual.shape
    gh = sends.shape[2]
    count = tiles.shape[0]
    f32 = jnp.float32
    dma = pltpu.SemaphoreType.DMA
    smem = pl.BlockSpec(memory_space=pltpu.SMEM)
    hbm = pl.BlockSpec(memory_space=pltpu.HBM)
    vmem = pl.BlockSpec(memory_space=pltpu.VMEM)
    scratch = (
        [pltpu.VMEM((split * own_rows + 2 * gh, cases, tb), f32)] * SENT
        + [pltpu.VMEM((own_rows, cases, tb), f32)] * (SENT + 3)
        + [pltpu.VMEM((2, gh, cases, tb), f32)] * SENT
        + [pltpu.VMEM((2, split, gh, cases, tb), f32)] * SENT
        + [
            pltpu.VMEM((count, tb, tb), f32),
            pltpu.VMEM((count // 2, 2 * tb, 2 * tb), jnp.bfloat16),
            pltpu.VMEM((3, cases, own_rows, tb), f32),
            pltpu.VMEM((split, cases, tb), f32),
            pltpu.VMEM((parts, cases, tb), f32),
            dma((4,)),
            dma((3,)),
            dma((SENT, split - 1)),
            dma((SENT, split - 1)),
            dma((SENT, 2, split)),
            dma((SENT, 2, split)),
            dma((split - 1,)),
            dma((split - 1,)),
            dma((parts - 1,)),
            dma((parts - 1,)),
        ]
    )
    out = jax.ShapeDtypeStruct((4, cases, own_rows, tb), f32)
    made = pl.pallas_call(
        functools.partial(kernel, parts, split),
        out_shape=out,
        in_specs=[smem] * 3 + [hbm] * 4,
        out_specs=vmem,
        scratch_shapes=scratch,
        compiler_params=pltpu.CompilerParams(
            collective_id=0, has_side_effects=True, vmem_limit_bytes=63 * 1024 * 1024
        ),
    )(rows, cols, sends, tiles, iterate, residual, direction)
    replaced = jnp.where(flags[:, None, None] > 0, right - made[1], made[2])
    return iterate + made[0], replaced, made[3]


def solution(mesh):
    both = ("dom", "rhs")
    vec = P(None, both, None)
    placed = (P(both, None, None), P(both), P(both), P("dom", None, None), P(), vec, vec, vec, vec)
    return jax.shard_map(
        functools.partial(body, mesh.shape["dom"], mesh.shape["rhs"]),
        mesh=mesh,
        in_specs=placed,
        out_specs=(vec, vec, vec),
        check_vma=False,
    )
```

```python
import functools

import jax
import jax.numpy as jnp
from jax import lax
from jax.experimental import pallas as pl
from jax.experimental.pallas import tpu as pltpu
from jax.sharding import PartitionSpec as P

SSTEP = 3
WIDTH = 2 * SSTEP + 1
P0, R0, X0, P1, R1, P2 = range(6)
SENT = 6
MESH = pl.DeviceIdType.MESH
UNROLL = 16
PAIRS = [(i, j) for i in range(WIDTH) for j in range(i, WIDTH)]
PAIR_LANE = {pair: lane for lane, pair in enumerate(PAIRS)}


def shifted_of(vec):
    return {i + 1: v for i, v in vec.items() if i not in (SSTEP, WIDTH - 1)}


def axpy(base, scale, other, sign):
    out = dict(base)
    for i, v in other.items():
        term = scale * v
        if i in out:
            out[i] = out[i] + term if sign > 0 else out[i] - term
        else:
            out[i] = term if sign > 0 else -term
    return out


def coefficients(gram):
    def quadratic(first, second):
        total = None
        for i, a in first.items():
            inner = None
            for j, b in second.items():
                term = gram[(min(i, j), max(i, j))] * b
                inner = term if inner is None else inner + term
            inner = inner * a
            total = inner if total is None else total + inner
        return total

    one = jnp.ones_like(gram[(0, 0)])
    direction = {0: one}
    residual = {SSTEP + 1: one}
    iterate = {}
    norm = quadratic(residual, residual)
    for _ in range(SSTEP):
        mapped = shifted_of(direction)
        step = norm / quadratic(direction, mapped)
        iterate = axpy(iterate, step, direction, 1)
        residual = axpy(residual, step, mapped, -1)
        next_norm = quadratic(residual, residual)
        direction = axpy(residual, next_norm / norm, direction, 1)
        norm = next_norm
    return iterate, residual, direction


def kernel(
    parts,
    split,
    rows_s,
    cols_s,
    sends_s,
    tiles_h,
    iterate_h,
    residual_h,
    direction_h,
    out_ref,
    *scratch,
):
    scratch = list(scratch)
    take = lambda n: [scratch.pop(0) for _ in range(n)]
    ext = take(SENT)
    own = take(SENT + 3)
    ghost_send = take(SENT)
    ghost_recv = take(SENT)
    tiles, weights, vec_in, gram_r, gram_d = take(5)
    tile_sem, vec_sem, peer_send, peer_recv, side_send, side_recv = take(6)
    gr_send, gr_recv, gd_send, gd_recv = take(4)

    d, r = lax.axis_index("dom"), lax.axis_index("rhs")
    cases, own_rows, tb = own[0].shape[1], own[0].shape[0], own[0].shape[2]
    gh = ghost_send[0].shape[1]
    tile_count = tiles.shape[0]
    chunks = tile_sem.shape[0]
    per_chunk = tile_count // chunks
    base = r * own_rows
    has_left, has_right = d > 0, d < parts - 1

    barrier = pltpu.get_barrier_semaphore()

    def greet(dd, rr):
        pl.semaphore_signal(barrier, inc=1, device_id=(dd, rr), device_id_type=MESH)

    @pl.loop(1, parts * split)
    def _(o):
        to = lax.rem(d * split + r + o, parts * split)
        greet(to // split, lax.rem(to, split))

    vec_copies = []
    for i, ref in enumerate((direction_h, residual_h, iterate_h)):
        copy = pltpu.make_async_copy(ref, vec_in.at[i], vec_sem.at[i])
        copy.start()
        vec_copies.append(copy)
    tile_copies = []
    for i in range(chunks):
        part = pl.ds(i * per_chunk, per_chunk)
        copy = pltpu.make_async_copy(tiles_h.at[part], tiles.at[part], tile_sem.at[i])
        copy.start()
        tile_copies.append(copy)

    sides = has_left.astype(jnp.int32) + has_right.astype(jnp.int32)

    def peer_copy(v, o):
        return pltpu.make_async_remote_copy(
            src_ref=own[v],
            dst_ref=ext[v].at[pl.ds(base, own_rows)],
            send_sem=peer_send.at[v, o - 1],
            recv_sem=peer_recv.at[v, o - 1],
            device_id=(d, lax.rem(r + o, split)),
            device_id_type=MESH,
        )

    def side_copy(v, side, o):
        return pltpu.make_async_remote_copy(
            src_ref=ghost_send[v].at[side],
            dst_ref=ghost_recv[v].at[1 - side, o],
            send_sem=side_send.at[v, side, o],
            recv_sem=side_recv.at[v, 1 - side, o],
            device_id=(d - 1 if side == 0 else d + 1, lax.rem(r + o, split)),
            device_id_type=MESH,
        )

    def stage(v, values):
        for b in range(own_rows):
            own[v][b] = values[b]
            ext[v][base + b] = values[b]
        for side in range(2):
            for k in range(gh):
                local = sends_s[0, side, k] - base
                value = own[v][jnp.clip(local, 0, own_rows - 1)]
                where = jnp.full((cases, tb), local, jnp.int32)
                ghost_send[v][side, k] = jnp.where(
                    (where >= 0) & (where < own_rows), value, 0.0
                )

    def send(v):
        @pl.when(has_left)
        def _():
            for o in range(split):
                side_copy(v, 0, o).start()

        @pl.when(has_right)
        def _():
            for o in range(split):
                side_copy(v, 1, o).start()

        for o in range(1, split):
            peer_copy(v, o).start()

    def receive(v):
        for o in range(1, split):
            peer_copy(v, o).wait_recv()
        for side, present in ((0, has_left), (1, has_right)):
            first = split * own_rows + side * gh

            @pl.when(present)
            def _():
                for o in range(split):
                    side_copy(v, 1 - side, o).wait_recv()
                for k in range(gh):
                    total = ghost_recv[v][side, 0, k]
                    for o in range(1, split):
                        total = total + ghost_recv[v][side, o, k]
                    ext[v][first + k] = total

            @pl.when(jnp.logical_not(present))
            def _():
                for k in range(gh):
                    ext[v][first + k] = jnp.zeros((cases, tb), jnp.float32)

    def sent(v):
        for o in range(1, split):
            peer_copy(v, o).wait_send()
        for side, present in ((0, has_left), (1, has_right)):

            @pl.when(present)
            def _():
                for o in range(split):
                    side_copy(v, side, o).wait_send()

    def input_blocks(i):
        return [vec_in[i, :, b, :] for b in range(own_rows)]

    low = lax.broadcasted_iota(jnp.int32, (2 * cases, tb), 0) < cases

    def apply_to(v):
        def step(i, acc):
            acc = list(acc)
            for u in range(UNROLL):
                q = i * UNROLL + u
                pair = jnp.concatenate(
                    [ext[v][cols_s[2 * q]], ext[v][cols_s[2 * q + 1]]], axis=0
                )
                high = pair.astype(jnp.bfloat16).astype(jnp.float32)
                lhs = jnp.concatenate([high, pair - high], axis=0).astype(jnp.bfloat16)
                lhs = jnp.concatenate([lhs, lhs], axis=1)
                out = jnp.dot(lhs, weights[q], preferred_element_type=jnp.float32)
                out = out[: 2 * cases] + out[2 * cases :]
                out = jnp.where(low, out[:, :tb], out[:, tb:])
                row = jnp.where(low, rows_s[2 * q], rows_s[2 * q + 1]) - base
                acc = [a + jnp.where(row == b, out, 0.0) for b, a in enumerate(acc)]
            return tuple(acc)

        zero = jnp.zeros((2 * cases, tb), jnp.float32)
        acc = lax.fori_loop(0, tile_count // 2 // UNROLL, step, (zero,) * own_rows)
        return [a[:cases] + a[cases:] for a in acc]

    for v in range(3):
        vec_copies[v].wait()
        stage(v, input_blocks(v))
    pl.semaphore_wait(barrier, parts * split - 1)
    send(P0)
    send(R0)

    for i in range(chunks):
        tile_copies[i].wait()

        @pl.loop(i * per_chunk // 2, (i + 1) * per_chunk // 2)
        def _(q):
            for h in range(2):
                flipped = tiles[2 * q + h].T
                high = flipped.astype(jnp.bfloat16)
                weights[q, :tb, h * tb : (h + 1) * tb] = high
                weights[q, tb:, h * tb : (h + 1) * tb] = (
                    flipped - high.astype(jnp.float32)
                ).astype(jnp.bfloat16)

    lanes = lax.broadcasted_iota(jnp.int32, (cases, tb), 1)
    basis = [own[P0], own[P1], own[P2], own[SENT], own[R0], own[R1], own[SENT + 1]]
    image = own[SENT + 2]

    def gram_of(payload, pairs):
        for i, j in pairs:
            total = basis[i][0] * basis[j][0]
            for b in range(1, own_rows):
                total = total + basis[i][b] * basis[j][b]
            total = jnp.sum(total, axis=1, keepdims=True)
            payload = payload + jnp.where(lanes == PAIR_LANE[(i, j)], total, 0.0)
        return payload

    def pairs_new(known, new):
        have = set(known) | set(new)
        return [p for p in PAIRS if set(p) <= have and set(p) & set(new)]

    receive(P0)
    stage(P1, apply_to(P0))
    send(P1)
    receive(R0)
    stage(R1, apply_to(R0))
    send(R1)
    send(X0)
    payload = jnp.zeros((cases, tb), jnp.float32)
    payload = gram_of(payload, pairs_new([], [0, 1, 4, 5]))
    receive(P1)
    stage(P2, apply_to(P1))
    send(P2)
    receive(R1)
    for b, value in enumerate(apply_to(R1)):
        own[SENT + 1][b] = value
    receive(X0)
    for b, value in enumerate(apply_to(X0)):
        image[b] = value
    payload = gram_of(payload, pairs_new([0, 1, 4, 5], [2, 6]))
    receive(P2)
    for b, value in enumerate(apply_to(P2)):
        own[SENT][b] = value
    payload = gram_of(payload, pairs_new([0, 1, 2, 4, 5, 6], [3]))

    me = d * split + r
    gram_d[me] = payload

    def gram_d_copy(o):
        to = lax.rem(me + o, parts * split)
        return pltpu.make_async_remote_copy(
            src_ref=gram_d.at[me],
            dst_ref=gram_d.at[me],
            send_sem=gd_send.at[o - 1],
            recv_sem=gd_recv.at[o - 1],
            device_id=(to // split, lax.rem(to, split)),
            device_id_type=MESH,
        )

    @pl.loop(1, parts * split)
    def _(o):
        gram_d_copy(o).start()

    for v in range(SENT):
        sent(v)

    @pl.loop(1, parts * split)
    def _(o):
        gram_d_copy(o).wait()

    whole = jnp.sum(gram_d[...], axis=0)
    gram = {
        pair: jnp.broadcast_to(whole[:, lane : lane + 1], (cases, tb))
        for pair, lane in PAIR_LANE.items()
    }
    iterate_c, residual_c, direction_c = coefficients(gram)
    shifted_c = shifted_of(iterate_c)
    for b in range(own_rows):
        blocks = [ref[b] for ref in basis]

        def combine(weights_of):
            total = None
            for i, w in weights_of.items():
                total = blocks[i] * w if total is None else total + blocks[i] * w
            return total

        out_ref[0, :, b, :] = combine(iterate_c)
        out_ref[1, :, b, :] = image[b] + combine(shifted_c)
        out_ref[2, :, b, :] = combine(residual_c)
        out_ref[3, :, b, :] = combine(direction_c)


def body(parts, split, tiles, rows, cols, sends, flags, right, iterate, residual, direction):
    cases, own_rows, tb = residual.shape
    gh = sends.shape[2]
    count = tiles.shape[0]
    f32 = jnp.float32
    dma = pltpu.SemaphoreType.DMA
    smem = pl.BlockSpec(memory_space=pltpu.SMEM)
    hbm = pl.BlockSpec(memory_space=pltpu.HBM)
    vmem = pl.BlockSpec(memory_space=pltpu.VMEM)
    scratch = (
        [pltpu.VMEM((split * own_rows + 2 * gh, cases, tb), f32)] * SENT
        + [pltpu.VMEM((own_rows, cases, tb), f32)] * (SENT + 3)
        + [pltpu.VMEM((2, gh, cases, tb), f32)] * SENT
        + [pltpu.VMEM((2, split, gh, cases, tb), f32)] * SENT
        + [
            pltpu.VMEM((count, tb, tb), f32),
            pltpu.VMEM((count // 2, 2 * tb, 2 * tb), jnp.bfloat16),
            pltpu.VMEM((3, cases, own_rows, tb), f32),
            pltpu.VMEM((split, cases, tb), f32),
            pltpu.VMEM((parts * split, cases, tb), f32),
            dma((4,)),
            dma((3,)),
            dma((SENT, split - 1)),
            dma((SENT, split - 1)),
            dma((SENT, 2, split)),
            dma((SENT, 2, split)),
            dma((split - 1,)),
            dma((split - 1,)),
            dma((parts * split - 1,)),
            dma((parts * split - 1,)),
        ]
    )
    out = jax.ShapeDtypeStruct((4, cases, own_rows, tb), f32)
    made = pl.pallas_call(
        functools.partial(kernel, parts, split),
        out_shape=out,
        in_specs=[smem] * 3 + [hbm] * 4,
        out_specs=vmem,
        scratch_shapes=scratch,
        compiler_params=pltpu.CompilerParams(
            collective_id=0, has_side_effects=True, vmem_limit_bytes=63 * 1024 * 1024
        ),
    )(rows, cols, sends, tiles, iterate, residual, direction)
    replaced = jnp.where(flags[:, None, None] > 0, right - made[1], made[2])
    return iterate + made[0], replaced, made[3]


def solution(mesh):
    both = ("dom", "rhs")
    vec = P(None, both, None)
    placed = (P(both, None, None), P(both), P(both), P("dom", None, None), P(), vec, vec, vec, vec)
    return jax.shard_map(
        functools.partial(body, mesh.shape["dom"], mesh.shape["rhs"]),
        mesh=mesh,
        in_specs=placed,
        out_specs=(vec, vec, vec),
        check_vma=False,
    )
```
